128 devices in a mesh: outer: 4 (over x), ctr: 32 (over y, z, core).
Axes of the slice: x: 4, y: 4, z: 4, core: 2. Of those that a mesh axis runs over, the one named last changes fastest.
Arguments:
- amplitudes: float32 [1024, 131072], P(('outer', 'ctr')), may hold values from -24 to 24
- integrals: float32 [4096, 131072], P('outer', 'ctr'), may hold values from -0.015625 to 0.015625
- block_mask: int32 [32, 1024], P('outer', 'ctr'), may hold values 0 or 1
Outputs:
- ladder: float32 [1024, 4096], P('ctr', 'outer')
The draws below stay inside these ranges and needn't reach their ends.
All inputs are finite; a program needn't handle non-finite values. No bound on the sum of `block_mask` on one device may be relied on, other than what follows from the above.
Results may differ from the reference program's by a relative error of at most 0.000071.
Values sent between devices are 32-bit elements; how exact they have to be, the bound alone decides.
A program may use at most 128 MiB of HBM per device.

```python
import jax
import jax.numpy as jnp
from jax import lax

TILE = 128
IJ = 1024
NAB = 32
NCD = 1024


def set_ends(drawn, rng, smallest, high):
    index_at = [jax.random.randint(jax.random.fold_in(rng, axis), (), 0, length) for axis, length in enumerate(drawn.shape)]
    longest = drawn.shape.index(max(drawn.shape))
    neighbour = index_at[:longest] + [(index_at[longest] + 1) % drawn.shape[longest]] + index_at[longest + 1:]
    return drawn.at[tuple(index_at)].set(smallest).at[tuple(neighbour)].set(high)


def with_spikes(entries, stream_key, source, target, blocks, factor):
    owner, partner = [(jnp.arange(entries.shape[position]) // (entries.shape[position] // blocks)).reshape([-1 if axis == position else 1 for axis in range(entries.ndim)]) for position in (source, target)]
    chosen = jax.random.permutation(stream_key, blocks)[partner]
    strong = (owner == chosen) | (owner == (partner + blocks // 2) % blocks)
    return jnp.where(strong, factor * entries, entries)


def steps_of(rng, extent, pieces, least, high):
    def one(axis_at, blocks):
        steps = jax.random.uniform(jax.random.fold_in(jax.random.fold_in(rng, 6), axis_at), (blocks,), jnp.float32, least / len(pieces), high / len(pieces))
        return jnp.repeat(jnp.exp(steps), extent[axis_at] // blocks).reshape((-1,) + (1,) * (len(extent) - axis_at - 1))

    factor_of = one(*pieces[0])
    for cut in pieces[1:]:
        factor_of = factor_of * one(*cut)
    return factor_of


def centred(rng, extent, spread, most, shards=(), held_as=jnp.bfloat16):
    result = spread * jax.random.normal(rng, extent, jnp.float32)
    if shards:
        result = result * steps_of(rng, extent, shards, -0.22, 0.18)
    return jnp.clip(result, -most, most).astype(held_as)


def gaussian_with(key, shape, width, reach, split, heavy, kind=jnp.bfloat16):
    drawn = width * jax.random.normal(key, shape, jnp.float32)
    if split:
        drawn = drawn * steps_of(key, shape, split, -0.22, 0.18)
    return jnp.clip(with_spikes(drawn, jax.random.fold_in(key, 3), *heavy), -reach, reach).astype(kind)


def setup_inputs(seed: int = 0) -> dict:
    key_list = jax.random.split(jax.random.key(seed), 4)
    return {
        "amplitudes": gaussian_with(key_list[0], (IJ, NCD * TILE), 1.0, 24.0, ((0, 128),), (1, 0, 128, 5.5), jnp.float32),
        "integrals": centred(key_list[1], (NAB * TILE, NCD * TILE), (NCD * TILE) ** -0.5, 0.015625, ((0, 4), (1, 32)), jnp.float32),
        "block_mask": set_ends((jax.random.randint(key_list[2], (NAB, NCD), 0, 5) < 3).astype(jnp.int32), jax.random.fold_in(key_list[2], 1), 0, 1),
    }


def reference(amplitudes, integrals, block_mask):
    mask_f = block_mask.astype(jnp.float32)
    rows = integrals.reshape(NAB, TILE, NCD * TILE)

    def one_block(pair):
        slab, mrow = pair
        wide = jnp.repeat(mrow, TILE)
        sparse_v = slab * wide[None, :]
        return lax.dot_general(amplitudes, sparse_v, (((1,), (1,)), ((), ())), precision=lax.Precision.HIGHEST, preferred_element_type=jnp.float32)

    parts = lax.map(one_block, (rows, mask_f))
    return jnp.transpose(parts, (1, 0, 2)).reshape(IJ, NAB * TILE)
```

```python
import functools

import jax
import jax.numpy as jnp
from jax import lax
from jax.experimental import pallas as pl
from jax.experimental.pallas import tpu as pltpu
from jax.sharding import PartitionSpec as P

MESH = pl.DeviceIdType.MESH
F32 = jnp.float32
BF16 = jnp.bfloat16
ROWS = 8
COLS = 4096
TILE = 128
AB = 1024
CHUNKS = 8
QUART = COLS // 4
UNITS = 4 * CHUNKS
AHEAD = 3
LAG = 7
NT = 256


def body(amp, integ, mask, out, t, vhi, vlo, stage, acc, land, own_sem, v_sem,
         a_send, a_recv, d_send, d_recv, f_send, f_recv, r_send, r_recv):
    o = lax.axis_index("outer")
    c = lax.axis_index("ctr")
    y = c // 8
    z = lax.rem(c // 2, 4)
    k = lax.rem(c, 2)
    right = lax.rem(o + 1, 4)
    left = lax.rem(o + 3, 4)

    def v_copy(v):
        return pltpu.make_async_copy(
            integ.at[pl.ds(v * TILE, TILE), :], stage.at[v % 2], v_sem.at[v % 2])

    v_copy(0).start()
    v_copy(1).start()

    barrier = pltpu.get_barrier_semaphore()
    for i in range(1, 32):
        pl.semaphore_signal(barrier, inc=1, device_id={"outer": o, "ctr": lax.rem(c + i, 32)}, device_id_type=MESH)
    for x in (right, left):
        pl.semaphore_signal(barrier, inc=1, device_id={"outer": x, "ctr": c}, device_id_type=MESH)
    pl.semaphore_wait(barrier, 33)

    def cols_of(ctr):
        return pl.ds(pl.multiple_of(ctr * COLS, COLS), COLS)

    def a_copy(q, core):
        to = lax.rem(y + 4 - q // 4, 4) * 8 + lax.rem(z + 4 - lax.rem(q, 4), 4) * 2 + core
        return pltpu.make_async_remote_copy(
            src_ref=amp.at[:, cols_of(to)],
            dst_ref=t.at[q // 2, 0, lax.rem(q, 2) * 2 + k],
            send_sem=a_send.at[2 * q + core],
            recv_sem=a_recv.at[2 * q + k],
            device_id={"outer": o, "ctr": to}, device_id_type=MESH)

    def a_wait(slot):
        pltpu.make_async_copy(
            t.at[0, 0, 0], t.at[slot // 4, 0, lax.rem(slot, 4)], a_recv.at[slot]).wait()

    own = pltpu.make_async_copy(amp.at[:, cols_of(c)], t.at[0, 0, k], own_sem)
    own.start()

    def x_copy(src, dst, sems, recvs, u, d):
        return pltpu.make_async_remote_copy(
            src_ref=src, dst_ref=dst, send_sem=sems.at[u, d], recv_sem=recvs.at[u, d],
            device_id={"outer": (right, left)[d], "ctr": c}, device_id_type=MESH)

    def quart(u):
        return pl.ds(pl.multiple_of(lax.rem(u, 4) * QUART, QUART), QUART)

    def direct(u, d, first=False):
        if first:
            slot = k if u == 0 else 1 - k if u == 1 else u
            src = amp.at[:, cols_of(c)] if u == 0 else t.at[0, 0, slot]
            return x_copy(src, t.at[0, (3, 1)[d], slot], d_send, d_recv, u, d)
        ch = u // 4
        return x_copy(t.at[ch, 0, :, :, quart(u)], t.at[ch, (3, 1)[d], :, :, quart(u)], d_send, d_recv, u, d)

    def forward(u, d, first=False):
        if first:
            slot = k if u == 0 else 1 - k if u == 1 else u
            half = pl.ds(d * (COLS // 2), COLS // 2)
            return x_copy(t.at[0, (3, 1)[d], slot, :, half], t.at[0, 2, slot, :, half], f_send, f_recv, u, d)
        ch = u // 4
        two = pl.ds(2 * d, 2)
        return x_copy(t.at[ch, (3, 1)[d], two, :, quart(u)], t.at[ch, 2, two, :, quart(u)], f_send, f_recv, u, d)

    def vprep(v):
        v_copy(v).wait()

        @pl.loop(0, COLS // TILE)
        def _(b):
            at = pl.ds(pl.multiple_of(b * TILE, TILE), TILE)
            m = mask[v, b].astype(F32)
            x = stage[v % 2, :, at] * m
            hi = x.astype(BF16)
            lo = (x - hi.astype(F32)).astype(BF16)
            vhi[pl.ds(v * TILE, TILE), at] = hi
            vlo[pl.ds(v * TILE, TILE), at] = lo

        if v + 2 < AB // TILE:
            v_copy(v + 2).start()

    def multiply(u):
        ch = u // 4
        rows = t[ch, :, :, :, quart(u)].reshape(4 * 4 * ROWS, QUART)
        hi = rows.astype(BF16)
        lo = (rows - hi.astype(F32)).astype(BF16)
        both = jnp.concatenate([hi, lo], axis=0)
        dims = (((1,), (1,)), ((), ()))

        @pl.loop(0, AB // NT)
        def _(n):
            at = pl.ds(pl.multiple_of(n * NT, NT), NT)
            a = lax.dot_general(both, vhi[at, quart(u)], dims, preferred_element_type=F32)
            b = lax.dot_general(hi, vlo[at, quart(u)], dims, preferred_element_type=F32)
            p = a[:128] + a[128:] + b
            p = p.reshape(16, ROWS, NT)

            @pl.when(lax.rem(u, 4) == 0)
            def _():
                acc[ch, :, :, at] = p

            @pl.when(lax.rem(u, 4) != 0)
            def _():
                acc[ch, :, :, at] += p

    def spread(ch, p, h):
        q = 2 * ch + h
        ys = lax.rem(y + q // 4, 4)
        zs = lax.rem(z + lax.rem(q, 4), 4)
        to = 8 * lax.rem(o + p, 4) + 2 * ys + zs // 2
        src = acc.at[ch, pl.ds(4 * p + 2 * h, 2)]
        dst = land.at[c, pl.ds(2 * lax.rem(zs, 2), 2)]
        sem = r_send.at[8 * ch + 2 * p + h]
        return to, lax.rem(zs, 2), src, dst, sem

    def spread_start(ch):
        @pl.loop(0, 8)
        def _(i):
            to, b, src, dst, sem = spread(ch, i // 2, lax.rem(i, 2))

            @pl.when(to == c)
            def _():
                pltpu.make_async_copy(src, dst, sem).start()

            @pl.when(to != c)
            def _():
                pltpu.make_async_remote_copy(
                    src_ref=src, dst_ref=dst, send_sem=sem, recv_sem=r_recv.at[2 * c + b],
                    device_id={"outer": o, "ctr": to}, device_id_type=MESH).start()

    a_copy(0, 1 - k).start()
    for d in (0, 1):
        direct(0, d, True).start()

    @pl.loop(2, 32)
    def _(i):
        a_copy(i // 2, lax.rem(i, 2)).start()

    a_wait(1 - k)
    for d in (0, 1):
        direct(1, d, True).start()
    vprep(0)
    a_wait(2)
    for d in (0, 1):
        direct(2, d, True).start()

    for s in range(LAG):
        u = s + AHEAD
        if u < 4:
            a_wait(u)
            for d in (0, 1):
                direct(u, d, True).start()
        else:
            if u % 4 == 0:
                for j in range(4):
                    a_wait(u + j)
            for d in (0, 1):
                direct(u, d).start()
        for d in (0, 1):
            direct(s, d, s < 4).wait_recv()
            forward(s, d, s < 4).start()
        vprep(s + 1)
        if s >= 4:
            for d in (0, 1):
                forward(s - 4, d, s < 8).wait_recv()
    own.wait()

    @pl.loop(LAG, UNITS + LAG)
    def _(s):
        @pl.when(s < UNITS - AHEAD)
        def _():
            u = s + AHEAD

            @pl.when(lax.rem(u, 4) == 0)
            def _():
                for j in range(4):
                    a_wait(u + j)
            for d in (0, 1):
                direct(u, d).start()

        @pl.when(s < UNITS)
        def _():
            for d in (0, 1):
                direct(s, d).wait_recv()
                forward(s, d).start()

        @pl.when(s == LAG)
        def _():
            for d in (0, 1):
                forward(3, d, True).wait_recv()

        @pl.when((s > LAG) & (s < UNITS))
        def _():
            for d in (0, 1):
                forward(s - 4, d).wait_recv()

        @pl.when(s >= UNITS + LAG - 4)
        def _():
            for d in (0, 1):
                forward(s - LAG, d).wait_recv()
        u = s - LAG
        multiply(u)

        @pl.when(lax.rem(u, 4) == 3)
        def _():
            spread_start(u // 4)

    a_copy(0, 1 - k).wait_send()

    @pl.loop(2, 32)
    def _(i):
        a_copy(i // 2, lax.rem(i, 2)).wait_send()
    for u in range(4):
        for d in (0, 1):
            direct(u, d, True).wait_send()
            forward(u, d, True).wait_send()

    @pl.loop(4, UNITS)
    def _(u):
        for d in (0, 1):
            direct(u, d).wait_send()
            forward(u, d).wait_send()

    @pl.loop(0, 64)
    def _(i):
        _, _, src, dst, sem = spread(i // 8, lax.rem(i // 2, 4), lax.rem(i, 2))
        pltpu.make_async_copy(src, dst, sem).wait()

    @pl.loop(0, 64)
    def _(i):
        @pl.when(i // 2 != c)
        def _():
            piece = land.at[i // 2, pl.ds(2 * lax.rem(i, 2), 2)]
            pltpu.make_async_copy(piece, piece, r_recv.at[i]).wait()

    @pl.loop(0, 4)
    def _(r):
        total = land[0, r]
        for i in range(1, 32):
            total = total + land[i, r]
        out[pl.ds(pl.multiple_of(r * ROWS, ROWS), ROWS), :] = total


def local(amplitudes, integrals, block_mask):
    dma = pltpu.SemaphoreType.DMA
    return pl.pallas_call(
        body,
        name="ladder",
        out_shape=jax.ShapeDtypeStruct((4 * ROWS, AB), F32),
        in_specs=[
            pl.BlockSpec(memory_space=pl.ANY),
            pl.BlockSpec(memory_space=pl.ANY),
            pl.BlockSpec(memory_space=pltpu.SMEM),
        ],
        out_specs=pl.BlockSpec(memory_space=pltpu.VMEM),
        scratch_shapes=[
            pltpu.VMEM((CHUNKS, 4, 4, ROWS, COLS), F32),
            pltpu.VMEM((AB, COLS), BF16),
            pltpu.VMEM((AB, COLS), BF16),
            pltpu.VMEM((2, TILE, COLS), F32),
            pltpu.VMEM((CHUNKS, 16, ROWS, AB), F32),
            pltpu.VMEM((32, 4, ROWS, AB), F32),
            dma,
            dma((2,)),
            dma((32,)), dma((32,)),
            dma((UNITS, 2)), dma((UNITS, 2)),
            dma((UNITS, 2)), dma((UNITS, 2)),
            dma((64,)), dma((64,)),
        ],
        compiler_params=pltpu.CompilerParams(
            collective_id=0, has_side_effects=True, vmem_limit_bytes=64 * 2**20 - 65536),
    )(amplitudes, integrals, block_mask)


def solution(mesh):
    return jax.shard_map(
        local,
        mesh=mesh,
        in_specs=(P(("outer", "ctr"), None), P("outer", "ctr"), P("outer", "ctr")),
        out_specs=P("ctr", "outer"),
        check_vma=False,
    )
```

```python
import functools

import jax
import jax.numpy as jnp
from jax import lax
from jax.experimental import pallas as pl
from jax.experimental.pallas import tpu as pltpu
from jax.sharding import PartitionSpec as P

MESH = pl.DeviceIdType.MESH
F32 = jnp.float32
BF16 = jnp.bfloat16
ROWS = 8
COLS = 4096
TILE = 128
AB = 1024
CHUNKS = 8
QUART = COLS // 4
UNITS = 4 * CHUNKS
AHEAD = 3
LAG = 7
NT = 256


ORDER = ((0, 0), (0, 1), (0, 3), (1, 0), (3, 0), (1, 1), (3, 3), (1, 3),
         (3, 1), (0, 2), (2, 0), (1, 2), (3, 2), (2, 1), (2, 3), (2, 2))
DY = [a for a, _ in ORDER]
DZ = [b for _, b in ORDER]


def packed(table, q):
    if isinstance(q, int):
        return table[q]
    word = sum(value << (2 * i) for i, value in enumerate(table))
    word = word - 2**32 if word >= 2**31 else word
    return lax.bitwise_and(lax.shift_right_logical(jnp.int32(word), 2 * q), jnp.int32(3))


def body(amp, integ, mask, out, t, vhi, vlo, stage, acc, land, own_sem, v_sem,
         a_send, a_recv, d_send, d_recv, f_send, f_recv, r_send, r_recv):
    o = lax.axis_index("outer")
    c = lax.axis_index("ctr")
    y = c // 8
    z = lax.rem(c // 2, 4)
    k = lax.rem(c, 2)
    right = lax.rem(o + 1, 4)
    left = lax.rem(o + 3, 4)

    def v_copy(v):
        return pltpu.make_async_copy(
            integ.at[pl.ds(v * TILE, TILE), :], stage.at[v % 2], v_sem.at[v % 2])

    v_copy(0).start()
    v_copy(1).start()

    barrier = pltpu.get_barrier_semaphore()
    for i in range(1, 32):
        pl.semaphore_signal(barrier, inc=1, device_id={"outer": o, "ctr": lax.rem(c + i, 32)}, device_id_type=MESH)
    for x in (right, left):
        pl.semaphore_signal(barrier, inc=1, device_id={"outer": x, "ctr": c}, device_id_type=MESH)
    pl.semaphore_wait(barrier, 33)

    def cols_of(ctr):
        return pl.ds(pl.multiple_of(ctr * COLS, COLS), COLS)

    def offset(q):
        return packed(DY, q), packed(DZ, q)

    def a_copy(q, core):
        dy, dz = offset(q)
        to = lax.rem(y + 4 - dy, 4) * 8 + lax.rem(z + 4 - dz, 4) * 2 + core
        return pltpu.make_async_remote_copy(
            src_ref=amp.at[:, cols_of(to)],
            dst_ref=t.at[q // 2, 0, lax.rem(q, 2) * 2 + k],
            send_sem=a_send.at[2 * q + core],
            recv_sem=a_recv.at[2 * q + k],
            device_id={"outer": o, "ctr": to}, device_id_type=MESH)

    def a_wait(slot):
        pltpu.make_async_copy(
            t.at[0, 0, 0], t.at[slot // 4, 0, lax.rem(slot, 4)], a_recv.at[slot]).wait()

    own = pltpu.make_async_copy(amp.at[:, cols_of(c)], t.at[0, 0, k], own_sem)
    own.start()

    def x_copy(src, dst, sems, recvs, u, d):
        return pltpu.make_async_remote_copy(
            src_ref=src, dst_ref=dst, send_sem=sems.at[u, d], recv_sem=recvs.at[u, d],
            device_id={"outer": (right, left)[d], "ctr": c}, device_id_type=MESH)

    def quart(u):
        return pl.ds(pl.multiple_of(lax.rem(u, 4) * QUART, QUART), QUART)

    def direct(u, d, first=False):
        if first:
            slot = k if u == 0 else 1 - k if u == 1 else u
            src = amp.at[:, cols_of(c)] if u == 0 else t.at[0, 0, slot]
            return x_copy(src, t.at[0, (3, 1)[d], slot], d_send, d_recv, u, d)
        ch = u // 4
        return x_copy(t.at[ch, 0, :, :, quart(u)], t.at[ch, (3, 1)[d], :, :, quart(u)], d_send, d_recv, u, d)

    def forward(u, d, first=False):
        if first:
            slot = k if u == 0 else 1 - k if u == 1 else u
            half = pl.ds(d * (COLS // 2), COLS // 2)
            return x_copy(t.at[0, (3, 1)[d], slot, :, half], t.at[0, 2, slot, :, half], f_send, f_recv, u, d)
        ch = u // 4
        two = pl.ds(2 * d, 2)
        return x_copy(t.at[ch, (3, 1)[d], two, :, quart(u)], t.at[ch, 2, two, :, quart(u)], f_send, f_recv, u, d)

    def vprep(v):
        v_copy(v).wait()

        @pl.loop(0, COLS // TILE)
        def _(b):
            at = pl.ds(pl.multiple_of(b * TILE, TILE), TILE)
            m = mask[v, b].astype(F32)
            x = stage[v % 2, :, at] * m
            hi = x.astype(BF16)
            lo = (x - hi.astype(F32)).astype(BF16)
            vhi[pl.ds(v * TILE, TILE), at] = hi
            vlo[pl.ds(v * TILE, TILE), at] = lo

        if v + 2 < AB // TILE:
            v_copy(v + 2).start()

    def multiply(u):
        ch = u // 4
        rows = t[ch, :, :, :, quart(u)].reshape(4 * 4 * ROWS, QUART)
        hi = rows.astype(BF16)
        lo = (rows - hi.astype(F32)).astype(BF16)
        both = jnp.concatenate([hi, lo], axis=0)
        dims = (((1,), (1,)), ((), ()))

        @pl.loop(0, AB // NT)
        def _(n):
            at = pl.ds(pl.multiple_of(n * NT, NT), NT)
            a = lax.dot_general(both, vhi[at, quart(u)], dims, preferred_element_type=F32)
            b = lax.dot_general(hi, vlo[at, quart(u)], dims, preferred_element_type=F32)
            p = a[:128] + a[128:] + b
            p = p.reshape(16, ROWS, NT)

            @pl.when(lax.rem(u, 4) == 0)
            def _():
                acc[ch, :, :, at] = p

            @pl.when(lax.rem(u, 4) != 0)
            def _():
                acc[ch, :, :, at] += p

    def spread(ch, p, h):
        q = 2 * ch + h
        dy, dz = offset(q)
        ys = lax.rem(y + dy, 4)
        zs = lax.rem(z + dz, 4)
        to = 8 * lax.rem(o + p, 4) + 2 * ys + zs // 2
        src = acc.at[ch, pl.ds(4 * p + 2 * h, 2)]
        dst = land.at[c, pl.ds(2 * lax.rem(zs, 2), 2)]
        sem = r_send.at[8 * ch + 2 * p + h]
        return to, lax.rem(zs, 2), src, dst, sem

    def spread_start(ch):
        @pl.loop(0, 8)
        def _(i):
            to, b, src, dst, sem = spread(ch, i // 2, lax.rem(i, 2))

            @pl.when(to == c)
            def _():
                pltpu.make_async_copy(src, dst, sem).start()

            @pl.when(to != c)
            def _():
                pltpu.make_async_remote_copy(
                    src_ref=src, dst_ref=dst, send_sem=sem, recv_sem=r_recv.at[2 * c + b],
                    device_id={"outer": o, "ctr": to}, device_id_type=MESH).start()

    a_copy(0, 1 - k).start()
    for d in (0, 1):
        direct(0, d, True).start()

    def a_start(ch):
        for i in range(4):
            a_copy(2 * ch + i // 2, i % 2).start()

    for i in range(2, 10):
        a_copy(i // 2, i % 2).start()

    a_wait(1 - k)
    for d in (0, 1):
        direct(1, d, True).start()
    vprep(0)
    a_wait(2)
    for d in (0, 1):
        direct(2, d, True).start()

    for s in range(LAG):
        u = s + AHEAD
        if s == 0:
            for i in range(10, 12):
                a_copy(i // 2, i % 2).start()
        if s % 4 == 0 and s:
            a_start(s // 4 + 2)
        if u < 4:
            a_wait(u)
            for d in (0, 1):
                direct(u, d, True).start()
        else:
            if u % 4 == 0:
                for j in range(4):
                    a_wait(u + j)
            for d in (0, 1):
                direct(u, d).start()
        for d in (0, 1):
            direct(s, d, s < 4).wait_recv()
            forward(s, d, s < 4).start()
        vprep(s + 1)
        if s >= 4:
            for d in (0, 1):
                forward(s - 4, d, s < 8).wait_recv()
    own.wait()

    @pl.loop(LAG, UNITS + LAG)
    def _(s):
        @pl.when((lax.rem(s, 4) == 0) & (s <= 4 * (CHUNKS - 3)))
        def _():
            a_start(s // 4 + 2)

        @pl.when(s < UNITS - AHEAD)
        def _():
            u = s + AHEAD

            @pl.when(lax.rem(u, 4) == 0)
            def _():
                for j in range(4):
                    a_wait(u + j)
            for d in (0, 1):
                direct(u, d).start()

        @pl.when(s < UNITS)
        def _():
            for d in (0, 1):
                direct(s, d).wait_recv()
                forward(s, d).start()

        @pl.when(s == LAG)
        def _():
            for d in (0, 1):
                forward(3, d, True).wait_recv()

        @pl.when((s > LAG) & (s < UNITS))
        def _():
            for d in (0, 1):
                forward(s - 4, d).wait_recv()

        @pl.when(s >= UNITS + LAG - 4)
        def _():
            for d in (0, 1):
                forward(s - LAG, d).wait_recv()
        u = s - LAG
        multiply(u)

        @pl.when(lax.rem(u, 4) == 3)
        def _():
            spread_start(u // 4)

    a_copy(0, 1 - k).wait_send()

    @pl.loop(2, 32)
    def _(i):
        a_copy(i // 2, lax.rem(i, 2)).wait_send()
    for u in range(4):
        for d in (0, 1):
            direct(u, d, True).wait_send()
            forward(u, d, True).wait_send()

    @pl.loop(4, UNITS)
    def _(u):
        for d in (0, 1):
            direct(u, d).wait_send()
            forward(u, d).wait_send()

    @pl.loop(0, 64)
    def _(i):
        _, _, src, dst, sem = spread(i // 8, lax.rem(i // 2, 4), lax.rem(i, 2))
        pltpu.make_async_copy(src, dst, sem).wait()

    @pl.loop(0, 64)
    def _(i):
        @pl.when(i // 2 != c)
        def _():
            piece = land.at[i // 2, pl.ds(2 * lax.rem(i, 2), 2)]
            pltpu.make_async_copy(piece, piece, r_recv.at[i]).wait()

    @pl.loop(0, 4)
    def _(r):
        total = land[0, r]
        for i in range(1, 32):
            total = total + land[i, r]
        out[pl.ds(pl.multiple_of(r * ROWS, ROWS), ROWS), :] = total


def local(amplitudes, integrals, block_mask):
    dma = pltpu.SemaphoreType.DMA
    return pl.pallas_call(
        body,
        name="ladder",
        out_shape=jax.ShapeDtypeStruct((4 * ROWS, AB), F32),
        in_specs=[
            pl.BlockSpec(memory_space=pl.ANY),
            pl.BlockSpec(memory_space=pl.ANY),
            pl.BlockSpec(memory_space=pltpu.SMEM),
        ],
        out_specs=pl.BlockSpec(memory_space=pltpu.VMEM),
        scratch_shapes=[
            pltpu.VMEM((CHUNKS, 4, 4, ROWS, COLS), F32),
            pltpu.VMEM((AB, COLS), BF16),
            pltpu.VMEM((AB, COLS), BF16),
            pltpu.VMEM((2, TILE, COLS), F32),
            pltpu.VMEM((CHUNKS, 16, ROWS, AB), F32),
            pltpu.VMEM((32, 4, ROWS, AB), F32),
            dma,
            dma((2,)),
            dma((32,)), dma((32,)),
            dma((UNITS, 2)), dma((UNITS, 2)),
            dma((UNITS, 2)), dma((UNITS, 2)),
            dma((64,)), dma((64,)),
        ],
        compiler_params=pltpu.CompilerParams(
            collective_id=0, has_side_effects=True, vmem_limit_bytes=64 * 2**20 - 65536),
    )(amplitudes, integrals, block_mask)


def solution(mesh):
    return jax.shard_map(
        local,
        mesh=mesh,
        in_specs=(P(("outer", "ctr"), None), P("outer", "ctr"), P("outer", "ctr")),
        out_specs=P("ctr", "outer"),
        check_vma=False,
    )
```

```python
import functools

import jax
import jax.numpy as jnp
from jax import lax
from jax.experimental import pallas as pl
from jax.experimental.pallas import tpu as pltpu
from jax.sharding import PartitionSpec as P

MESH = pl.DeviceIdType.MESH
F32 = jnp.float32
BF16 = jnp.bfloat16
ROWS = 8
COLS = 4096
TILE = 128
AB = 1024
CHUNKS = 8
QUART = COLS // 4
UNITS = 4 * CHUNKS
AHEAD = 3
START = 7
LAG = 4
NT = 256


ORDER = ((0, 0), (0, 1), (0, 3), (1, 0), (3, 0), (1, 1), (3, 3), (1, 3),
         (3, 1), (0, 2), (2, 0), (1, 2), (3, 2), (2, 1), (2, 3), (2, 2))
DY = [a for a, _ in ORDER]
DZ = [b for _, b in ORDER]


def packed(table, q):
    if isinstance(q, int):
        return table[q]
    word = sum(value << (2 * i) for i, value in enumerate(table))
    word = word - 2**32 if word >= 2**31 else word
    return lax.bitwise_and(lax.shift_right_logical(jnp.int32(word), 2 * q), jnp.int32(3))


def body(amp, integ, mask, out, t, vhi, vlo, stage, acc, land, own_sem, v_sem,
         a_send, a_recv, d_send, d_recv, f_send, f_recv, r_send, r_recv):
    o = lax.axis_index("outer")
    c = lax.axis_index("ctr")
    y = c // 8
    z = lax.rem(c // 2, 4)
    k = lax.rem(c, 2)
    right = lax.rem(o + 1, 4)
    left = lax.rem(o + 3, 4)

    def v_copy(v):
        return pltpu.make_async_copy(
            integ.at[pl.ds(v * TILE, TILE), :], stage.at[v % 2], v_sem.at[v % 2])

    v_copy(0).start()
    v_copy(1).start()

    barrier = pltpu.get_barrier_semaphore()
    for i in range(1, 32):
        pl.semaphore_signal(barrier, inc=1, device_id={"outer": o, "ctr": lax.rem(c + i, 32)}, device_id_type=MESH)
    for x in (right, left):
        pl.semaphore_signal(barrier, inc=1, device_id={"outer": x, "ctr": c}, device_id_type=MESH)
    pl.semaphore_wait(barrier, 33)

    def cols_of(ctr):
        return pl.ds(pl.multiple_of(ctr * COLS, COLS), COLS)

    def offset(q):
        return packed(DY, q), packed(DZ, q)

    def a_copy(q, core):
        dy, dz = offset(q)
        to = lax.rem(y + 4 - dy, 4) * 8 + lax.rem(z + 4 - dz, 4) * 2 + core
        return pltpu.make_async_remote_copy(
            src_ref=amp.at[:, cols_of(to)],
            dst_ref=t.at[q // 2, 0, lax.rem(q, 2) * 2 + k],
            send_sem=a_send.at[2 * q + core],
            recv_sem=a_recv.at[2 * q + k],
            device_id={"outer": o, "ctr": to}, device_id_type=MESH)

    def a_wait(slot):
        pltpu.make_async_copy(
            t.at[0, 0, 0], t.at[slot // 4, 0, lax.rem(slot, 4)], a_recv.at[slot]).wait()

    own = pltpu.make_async_copy(amp.at[:, cols_of(c)], t.at[0, 0, k], own_sem)
    own.start()

    def x_copy(src, dst, sems, recvs, u, d):
        return pltpu.make_async_remote_copy(
            src_ref=src, dst_ref=dst, send_sem=sems.at[u, d], recv_sem=recvs.at[u, d],
            device_id={"outer": (right, left)[d], "ctr": c}, device_id_type=MESH)

    def quart(u):
        return pl.ds(pl.multiple_of(lax.rem(u, 4) * QUART, QUART), QUART)

    def direct(u, d, first=False):
        if first:
            slot = k if u == 0 else 1 - k if u == 1 else u
            src = amp.at[:, cols_of(c)] if u == 0 else t.at[0, 0, slot]
            return x_copy(src, t.at[0, (3, 1)[d], slot], d_send, d_recv, u, d)
        ch = u // 4
        return x_copy(t.at[ch, 0, :, :, quart(u)], t.at[ch, (3, 1)[d], :, :, quart(u)], d_send, d_recv, u, d)

    def forward(u, d, first=False):
        if first:
            slot = k if u == 0 else 1 - k if u == 1 else u
            half = pl.ds(d * (COLS // 2), COLS // 2)
            return x_copy(t.at[0, (3, 1)[d], slot, :, half], t.at[0, 2, slot, :, half], f_send, f_recv, u, d)
        ch = u // 4
        two = pl.ds(2 * d, 2)
        return x_copy(t.at[ch, (3, 1)[d], two, :, quart(u)], t.at[ch, 2, two, :, quart(u)], f_send, f_recv, u, d)

    def vprep(v):
        v_copy(v).wait()

        @pl.loop(0, COLS // TILE)
        def _(b):
            at = pl.ds(pl.multiple_of(b * TILE, TILE), TILE)
            m = mask[v, b].astype(F32)
            x = stage[v % 2, :, at] * m
            hi = x.astype(BF16)
            lo = (x - hi.astype(F32)).astype(BF16)
            vhi[pl.ds(v * TILE, TILE), at] = hi
            vlo[pl.ds(v * TILE, TILE), at] = lo

        if v + 2 < AB // TILE:
            v_copy(v + 2).start()

    def multiply(u):
        ch = u // 4
        rows = t[ch, :, :, :, quart(u)].reshape(4 * 4 * ROWS, QUART)
        hi = rows.astype(BF16)
        lo = (rows - hi.astype(F32)).astype(BF16)
        both = jnp.concatenate([hi, lo], axis=0)
        dims = (((1,), (1,)), ((), ()))

        @pl.loop(0, AB // NT)
        def _(n):
            at = pl.ds(pl.multiple_of(n * NT, NT), NT)
            a = lax.dot_general(both, vhi[at, quart(u)], dims, preferred_element_type=F32)
            b = lax.dot_general(hi, vlo[at, quart(u)], dims, preferred_element_type=F32)
            p = a[:128] + a[128:] + b
            p = p.reshape(16, ROWS, NT)

            @pl.when(lax.rem(u, 4) == 0)
            def _():
                acc[ch, :, :, at] = p

            @pl.when(lax.rem(u, 4) != 0)
            def _():
                acc[ch, :, :, at] += p

    def spread(ch, p, h):
        q = 2 * ch + h
        dy, dz = offset(q)
        ys = lax.rem(y + dy, 4)
        zs = lax.rem(z + dz, 4)
        to = 8 * lax.rem(o + p, 4) + 2 * ys + zs // 2
        src = acc.at[ch, pl.ds(4 * p + 2 * h, 2)]
        dst = land.at[c, pl.ds(2 * lax.rem(zs, 2), 2)]
        sem = r_send.at[8 * ch + 2 * p + h]
        return to, lax.rem(zs, 2), src, dst, sem

    def spread_start(ch):
        @pl.loop(0, 8)
        def _(i):
            to, b, src, dst, sem = spread(ch, i // 2, lax.rem(i, 2))

            @pl.when(to == c)
            def _():
                pltpu.make_async_copy(src, dst, sem).start()

            @pl.when(to != c)
            def _():
                pltpu.make_async_remote_copy(
                    src_ref=src, dst_ref=dst, send_sem=sem, recv_sem=r_recv.at[2 * c + b],
                    device_id={"outer": o, "ctr": to}, device_id_type=MESH).start()

    a_copy(0, 1 - k).start()
    for d in (0, 1):
        direct(0, d, True).start()

    def a_start(ch):
        for i in range(4):
            a_copy(2 * ch + i // 2, i % 2).start()

    for i in range(2, 10):
        a_copy(i // 2, i % 2).start()

    a_wait(1 - k)
    for d in (0, 1):
        direct(1, d, True).start()
    a_wait(2)
    for d in (0, 1):
        direct(2, d, True).start()

    for s in range(START):
        u = s + AHEAD
        if s == 0:
            for i in range(10, 12):
                a_copy(i // 2, i % 2).start()
        if s % 4 == 0 and s:
            a_start(s // 4 + 2)
        for d in (0, 1):
            direct(s, d, s < 4).wait_recv()
            forward(s, d, s < 4).start()
        if u < 4:
            a_wait(u)
            for d in (0, 1):
                direct(u, d, True).start()
        else:
            if u % 4 == 0:
                for j in range(4):
                    a_wait(u + j)
            for d in (0, 1):
                direct(u, d).start()
        vprep(s)
        if s >= 4:
            for d in (0, 1):
                forward(s - 4, d, s < 8).wait_recv()
    own.wait()
    vprep(START)

    @pl.loop(START, UNITS + LAG)
    def _(s):
        @pl.when((lax.rem(s, 4) == 0) & (s <= 4 * (CHUNKS - 3)))
        def _():
            a_start(s // 4 + 2)

        @pl.when(s < UNITS)
        def _():
            for d in (0, 1):
                direct(s, d).wait_recv()
                forward(s, d).start()

        @pl.when(s < UNITS - AHEAD)
        def _():
            u = s + AHEAD

            @pl.when(lax.rem(u, 4) == 0)
            def _():
                for j in range(4):
                    a_wait(u + j)
            for d in (0, 1):
                direct(u, d).start()

        @pl.when(s == START)
        def _():
            for d in (0, 1):
                forward(START - LAG, d, True).wait_recv()

        @pl.when(s > START)
        def _():
            for d in (0, 1):
                forward(s - LAG, d).wait_recv()

        first = jnp.minimum(2 * (s - START), s - LAG)
        last = jnp.minimum(2 * (s - START) + 2, s - LAG + 1)

        @pl.loop(first, last)
        def _(u):
            multiply(u)

            @pl.when(lax.rem(u, 4) == 3)
            def _():
                spread_start(u // 4)

    a_copy(0, 1 - k).wait_send()

    @pl.loop(2, 32)
    def _(i):
        a_copy(i // 2, lax.rem(i, 2)).wait_send()
    for u in range(4):
        for d in (0, 1):
            direct(u, d, True).wait_send()
            forward(u, d, True).wait_send()

    @pl.loop(4, UNITS)
    def _(u):
        for d in (0, 1):
            direct(u, d).wait_send()
            forward(u, d).wait_send()

    @pl.loop(0, 64)
    def _(i):
        _, _, src, dst, sem = spread(i // 8, lax.rem(i // 2, 4), lax.rem(i, 2))
        pltpu.make_async_copy(src, dst, sem).wait()

    @pl.loop(0, 64)
    def _(i):
        @pl.when(i // 2 != c)
        def _():
            piece = land.at[i // 2, pl.ds(2 * lax.rem(i, 2), 2)]
            pltpu.make_async_copy(piece, piece, r_recv.at[i]).wait()

    @pl.loop(0, 4)
    def _(r):
        total = land[0, r]
        for i in range(1, 32):
            total = total + land[i, r]
        out[pl.ds(pl.multiple_of(r * ROWS, ROWS), ROWS), :] = total


def local(amplitudes, integrals, block_mask):
    dma = pltpu.SemaphoreType.DMA
    return pl.pallas_call(
        body,
        name="ladder",
        out_shape=jax.ShapeDtypeStruct((4 * ROWS, AB), F32),
        in_specs=[
            pl.BlockSpec(memory_space=pl.ANY),
            pl.BlockSpec(memory_space=pl.ANY),
            pl.BlockSpec(memory_space=pltpu.SMEM),
        ],
        out_specs=pl.BlockSpec(memory_space=pltpu.VMEM),
        scratch_shapes=[
            pltpu.VMEM((CHUNKS, 4, 4, ROWS, COLS), F32),
            pltpu.VMEM((AB, COLS), BF16),
            pltpu.VMEM((AB, COLS), BF16),
            pltpu.VMEM((2, TILE, COLS), F32),
            pltpu.VMEM((CHUNKS, 16, ROWS, AB), F32),
            pltpu.VMEM((32, 4, ROWS, AB), F32),
            dma,
            dma((2,)),
            dma((32,)), dma((32,)),
            dma((UNITS, 2)), dma((UNITS, 2)),
            dma((UNITS, 2)), dma((UNITS, 2)),
            dma((64,)), dma((64,)),
        ],
        compiler_params=pltpu.CompilerParams(
            collective_id=0, has_side_effects=True, vmem_limit_bytes=64 * 2**20 - 65536),
    )(amplitudes, integrals, block_mask)


def solution(mesh):
    return jax.shard_map(
        local,
        mesh=mesh,
        in_specs=(P(("outer", "ctr"), None), P("outer", "ctr"), P("outer", "ctr")),
        out_specs=P("ctr", "outer"),
        check_vma=False,
    )
```

```python
import functools

import jax
import jax.numpy as jnp
from jax import lax
from jax.experimental import pallas as pl
from jax.experimental.pallas import tpu as pltpu
from jax.sharding import PartitionSpec as P

MESH = pl.DeviceIdType.MESH
F32 = jnp.float32
BF16 = jnp.bfloat16
ROWS = 8
COLS = 4096
TILE = 128
AB = 1024
CHUNKS = 8
QUART = COLS // 4
UNITS = 4 * CHUNKS
AHEAD = 3
START = 7
LAG = 4
NT = 256


ORDER = ((0, 0), (0, 1), (0, 3), (1, 0), (3, 0), (1, 1), (3, 3), (1, 3),
         (3, 1), (0, 2), (2, 0), (1, 2), (3, 2), (2, 1), (2, 3), (2, 2))
DY = [a for a, _ in ORDER]
DZ = [b for _, b in ORDER]


def packed(table, q):
    if isinstance(q, int):
        return table[q]
    word = sum(value << (2 * i) for i, value in enumerate(table))
    word = word - 2**32 if word >= 2**31 else word
    return lax.bitwise_and(lax.shift_right_logical(jnp.int32(word), 2 * q), jnp.int32(3))


def body(amp, integ, mask, out, t, vhi, vlo, stage, acc, land, own_sem, v_sem,
         a_send, a_recv, d_send, d_recv, f_send, f_recv, r_send, r_recv):
    o = lax.axis_index("outer")
    c = lax.axis_index("ctr")
    y = c // 8
    z = lax.rem(c // 2, 4)
    k = lax.rem(c, 2)
    right = lax.rem(o + 1, 4)
    left = lax.rem(o + 3, 4)

    def v_copy(v):
        return pltpu.make_async_copy(
            integ.at[pl.ds(v * TILE, TILE), :], stage.at[v % 2], v_sem.at[v % 2])

    v_copy(0).start()
    v_copy(1).start()

    barrier = pltpu.get_barrier_semaphore()
    for i in range(1, 32):
        pl.semaphore_signal(barrier, inc=1, device_id={"outer": o, "ctr": lax.rem(c + i, 32)}, device_id_type=MESH)
    for x in (right, left):
        pl.semaphore_signal(barrier, inc=1, device_id={"outer": x, "ctr": c}, device_id_type=MESH)
    pl.semaphore_wait(barrier, 33)

    def cols_of(ctr):
        return pl.ds(pl.multiple_of(ctr * COLS, COLS), COLS)

    def offset(q):
        return packed(DY, q), packed(DZ, q)

    def a_copy(q, core):
        dy, dz = offset(q)
        to = lax.rem(y + 4 - dy, 4) * 8 + lax.rem(z + 4 - dz, 4) * 2 + core
        return pltpu.make_async_remote_copy(
            src_ref=amp.at[:, cols_of(to)],
            dst_ref=t.at[q // 2, 0, lax.rem(q, 2) * 2 + k],
            send_sem=a_send.at[2 * q + core],
            recv_sem=a_recv.at[2 * q + k],
            device_id={"outer": o, "ctr": to}, device_id_type=MESH)

    def a_wait(slot):
        pltpu.make_async_copy(
            t.at[0, 0, 0], t.at[slot // 4, 0, lax.rem(slot, 4)], a_recv.at[slot]).wait()

    own = pltpu.make_async_copy(amp.at[:, cols_of(c)], t.at[0, 0, k], own_sem)
    own.start()

    def x_copy(src, dst, sems, recvs, u, d):
        return pltpu.make_async_remote_copy(
            src_ref=src, dst_ref=dst, send_sem=sems.at[u, d], recv_sem=recvs.at[u, d],
            device_id={"outer": (right, left)[d], "ctr": c}, device_id_type=MESH)

    def quart(u):
        return pl.ds(pl.multiple_of(lax.rem(u, 4) * QUART, QUART), QUART)

    def direct(u, d, first=False):
        if first:
            slot = k if u == 0 else 1 - k if u == 1 else u
            src = amp.at[:, cols_of(c)] if u == 0 else t.at[0, 0, slot]
            return x_copy(src, t.at[0, (3, 1)[d], slot], d_send, d_recv, u, d)
        ch = u // 4
        return x_copy(t.at[ch, 0, :, :, quart(u)], t.at[ch, (3, 1)[d], :, :, quart(u)], d_send, d_recv, u, d)

    def forward(u, d, first=False):
        if first:
            slot = k if u == 0 else 1 - k if u == 1 else u
            half = pl.ds(d * (COLS // 2), COLS // 2)
            return x_copy(t.at[0, (3, 1)[d], slot, :, half], t.at[0, 2, slot, :, half], f_send, f_recv, u, d)
        ch = u // 4
        two = pl.ds(2 * d, 2)
        return x_copy(t.at[ch, (3, 1)[d], two, :, quart(u)], t.at[ch, 2, two, :, quart(u)], f_send, f_recv, u, d)

    def vprep(v):
        v_copy(v).wait()

        @pl.loop(0, COLS // TILE)
        def _(b):
            at = pl.ds(pl.multiple_of(b * TILE, TILE), TILE)
            m = mask[v, b].astype(F32)
            x = stage[v % 2, :, at] * m
            hi = x.astype(BF16)
            lo = (x - hi.astype(F32)).astype(BF16)
            vhi[pl.ds(v * TILE, TILE), at] = hi
            vlo[pl.ds(v * TILE, TILE), at] = lo

        if v + 2 < AB // TILE:
            v_copy(v + 2).start()

    def multiply(u):
        ch = u // 4
        rows = t[ch, :, :, :, quart(u)].reshape(4 * 4 * ROWS, QUART)
        hi = rows.astype(BF16)
        lo = (rows - hi.astype(F32)).astype(BF16)
        both = jnp.concatenate([hi, lo], axis=0)
        dims = (((1,), (1,)), ((), ()))

        @pl.loop(0, AB // NT)
        def _(n):
            at = pl.ds(pl.multiple_of(n * NT, NT), NT)
            a = lax.dot_general(both, vhi[at, quart(u)], dims, preferred_element_type=F32)
            b = lax.dot_general(hi, vlo[at, quart(u)], dims, preferred_element_type=F32)
            p = a[:128] + a[128:] + b
            p = p.reshape(16, ROWS, NT)

            @pl.when(lax.rem(u, 4) == 0)
            def _():
                acc[ch, :, :, at] = p

            @pl.when(lax.rem(u, 4) != 0)
            def _():
                acc[ch, :, :, at] += p

    def spread(ch, p, h):
        q = 2 * ch + h
        dy, dz = offset(q)
        ys = lax.rem(y + dy, 4)
        zs = lax.rem(z + dz, 4)
        to = 8 * lax.rem(o + p, 4) + 2 * ys + zs // 2
        src = acc.at[ch, pl.ds(4 * p + 2 * h, 2)]
        dst = land.at[c, pl.ds(2 * lax.rem(zs, 2), 2)]
        sem = r_send.at[8 * ch + 2 * p + h]
        return to, lax.rem(zs, 2), src, dst, sem

    def spread_start(ch):
        @pl.loop(0, 8)
        def _(i):
            to, b, src, dst, sem = spread(ch, i // 2, lax.rem(i, 2))

            @pl.when(to == c)
            def _():
                pltpu.make_async_copy(src, dst, sem).start()

            @pl.when(to != c)
            def _():
                pltpu.make_async_remote_copy(
                    src_ref=src, dst_ref=dst, send_sem=sem, recv_sem=r_recv.at[2 * c + b],
                    device_id={"outer": o, "ctr": to}, device_id_type=MESH).start()

    a_copy(0, 1 - k).start()
    for d in (0, 1):
        direct(0, d, True).start()

    def a_start(ch):
        for i in range(4):
            a_copy(2 * ch + i // 2, i % 2).start()

    for i in range(2, 10):
        a_copy(i // 2, i % 2).start()

    a_wait(1 - k)
    for d in (0, 1):
        direct(1, d, True).start()
    vprep(0)
    a_wait(2)
    for d in (0, 1):
        direct(2, d, True).start()

    for s in range(START):
        u = s + AHEAD
        if s == 0:
            for i in range(10, 12):
                a_copy(i // 2, i % 2).start()
        if s % 4 == 0 and s:
            a_start(s // 4 + 2)
        if u < 4:
            a_wait(u)
            for d in (0, 1):
                direct(u, d, True).start()
        else:
            if u % 4 == 0:
                for j in range(4):
                    a_wait(u + j)
            for d in (0, 1):
                direct(u, d).start()
        for d in (0, 1):
            direct(s, d, s < 4).wait_recv()
            forward(s, d, s < 4).start()
        vprep(s + 1)
        if s >= 4:
            for d in (0, 1):
                forward(s - 4, d, s < 8).wait_recv()
    own.wait()

    @pl.loop(START, UNITS + LAG)
    def _(s):
        @pl.when((lax.rem(s, 4) == 0) & (s <= 4 * (CHUNKS - 3)))
        def _():
            a_start(s // 4 + 2)

        @pl.when(s < UNITS - AHEAD)
        def _():
            u = s + AHEAD

            @pl.when(lax.rem(u, 4) == 0)
            def _():
                for j in range(4):
                    a_wait(u + j)
            for d in (0, 1):
                direct(u, d).start()

        @pl.when(s < UNITS)
        def _():
            for d in (0, 1):
                direct(s, d).wait_recv()
                forward(s, d).start()

        @pl.when(s == START)
        def _():
            for d in (0, 1):
                forward(START - LAG, d, True).wait_recv()

        @pl.when(s > START)
        def _():
            for d in (0, 1):
                forward(s - LAG, d).wait_recv()

        first = jnp.minimum(2 * (s - START), s - LAG)
        last = jnp.minimum(2 * (s - START) + 2, s - LAG + 1)

        @pl.loop(first, last)
        def _(u):
            multiply(u)

            @pl.when(lax.rem(u, 4) == 3)
            def _():
                spread_start(u // 4)

    a_copy(0, 1 - k).wait_send()

    @pl.loop(2, 32)
    def _(i):
        a_copy(i // 2, lax.rem(i, 2)).wait_send()
    for u in range(4):
        for d in (0, 1):
            direct(u, d, True).wait_send()
            forward(u, d, True).wait_send()

    @pl.loop(4, UNITS)
    def _(u):
        for d in (0, 1):
            direct(u, d).wait_send()
            forward(u, d).wait_send()

    @pl.loop(0, 64)
    def _(i):
        _, _, src, dst, sem = spread(i // 8, lax.rem(i // 2, 4), lax.rem(i, 2))
        pltpu.make_async_copy(src, dst, sem).wait()

    @pl.loop(0, 64)
    def _(i):
        @pl.when(i // 2 != c)
        def _():
            piece = land.at[i // 2, pl.ds(2 * lax.rem(i, 2), 2)]
            pltpu.make_async_copy(piece, piece, r_recv.at[i]).wait()

    @pl.loop(0, 4)
    def _(r):
        total = land[0, r]
        for i in range(1, 32):
            total = total + land[i, r]
        out[pl.ds(pl.multiple_of(r * ROWS, ROWS), ROWS), :] = total


def local(amplitudes, integrals, block_mask):
    dma = pltpu.SemaphoreType.DMA
    return pl.pallas_call(
        body,
        name="ladder",
        out_shape=jax.ShapeDtypeStruct((4 * ROWS, AB), F32),
        in_specs=[
            pl.BlockSpec(memory_space=pl.ANY),
            pl.BlockSpec(memory_space=pl.ANY),
            pl.BlockSpec(memory_space=pltpu.SMEM),
        ],
        out_specs=pl.BlockSpec(memory_space=pltpu.VMEM),
        scratch_shapes=[
            pltpu.VMEM((CHUNKS, 4, 4, ROWS, COLS), F32),
            pltpu.VMEM((AB, COLS), BF16),
            pltpu.VMEM((AB, COLS), BF16),
            pltpu.VMEM((2, TILE, COLS), F32),
            pltpu.VMEM((CHUNKS, 16, ROWS, AB), F32),
            pltpu.VMEM((32, 4, ROWS, AB), F32),
            dma,
            dma((2,)),
            dma((32,)), dma((32,)),
            dma((UNITS, 2)), dma((UNITS, 2)),
            dma((UNITS, 2)), dma((UNITS, 2)),
            dma((64,)), dma((64,)),
        ],
        compiler_params=pltpu.CompilerParams(
            collective_id=0, has_side_effects=True, vmem_limit_bytes=64 * 2**20 - 65536),
    )(amplitudes, integrals, block_mask)


def solution(mesh):
    return jax.shard_map(
        local,
        mesh=mesh,
        in_specs=(P(("outer", "ctr"), None), P("outer", "ctr"), P("outer", "ctr")),
        out_specs=P("ctr", "outer"),
        check_vma=False,
    )
```
